32 devices in a mesh: inst: 4 (over x, core), space: 8 (over z, y).
Axes of the slice: x: 2, y: 2, z: 4, core: 2. Of those that a mesh axis runs over, the one named last changes fastest.
Arguments:
- adjoint_old: float32 [8, 6, 512, 512], P('inst', None, 'space'), may hold values from -6 to 6
- source_term: float32 [8, 6, 512, 512], P('inst', None, 'space'), may hold values from -6 to 6
- face_stream: float32 [8, 512, 512], P('inst', 'space'), may hold values from 0.2 to 1
- face_pitch: float32 [8, 512, 512], P('inst', 'space'), may hold values from 0.2 to 1
- diag_scale: float32 [8, 512, 512], P('inst', 'space'), may hold values from 0.1 to 0.4
- volume: float32 [512, 512], P('space'), may hold values from 0.5 to 2
- face_blocks: float32 [4, 6, 6], replicated, may hold values from -2.5 to 2.5
- diag_inverse: float32 [8, 6, 6], P('inst')
- periodic_block: float32 [6, 6], replicated, may hold values from -2.5 to 2.5
- frequency: float32 [1], replicated, may hold values from 0.5 to 2
- phase_shift: int32 [1], replicated, may hold values from 1 to 7
- periodic_cells: int32 [8, 8, 128], P('space'), may hold values from 0 to 32767
- periodic_targets: int32 [8, 8, 128], P(None, 'space'), may hold values from 0 to 32767
- periodic_weights: float32 [8, 8, 128], P('space'), may hold values from 0.5 to 1.5
- periodic_counts: int32 [8, 8], P('space'), may hold values from 0 to 128, as said below
Outputs:
- adjoint_new: float32 [8, 6, 512, 512], P('inst', None, 'space')
- residual: float32 [8, 6, 512, 512], P('inst', None, 'space')
The draws below stay inside these ranges and needn't reach their ends.
Inputs may be any that keep to these rules, and one draw needn't show every extreme that they name: `periodic_counts`: each partition's row has one peer with 128 live faces, and one partition receives 128 live faces from every partition. `periodic_cells`: local cell indices in the sending partition. `periodic_targets`: local cell indices in the receiving partition.
All inputs are finite; a program needn't handle non-finite values.
Results may differ from the reference program's by a relative error of at most 0.0001.
Values sent between devices are 32-bit elements; how exact they have to be, the bound alone decides.
A program may use at most 128 MiB of HBM per device.

```python
import math
import jax
import jax.numpy as jnp
from jax import lax

VARS = 6
CI = 64
NJ = 512
PSLOT = 128
SWEEPS = 2
INSTANCES = 8
NI = 512
N_SPACE = 8


def draw_diag_inverse(key, part):
    noise = jax.random.normal(key, (INSTANCES, VARS, VARS), jnp.float32) * 0.5
    return jnp.eye(VARS, dtype=jnp.float32)[None] + noise / math.sqrt(VARS)


def draw_periodic_counts(key, part):
    first = jax.random.fold_in(key, 11)
    second = jax.random.fold_in(key, 12)
    third = jax.random.fold_in(key, 13)
    counts = jax.random.randint(first, (N_SPACE, N_SPACE), 0, PSLOT + 1)
    peers = jax.random.permutation(second, N_SPACE)
    counts = counts.at[jnp.arange(N_SPACE), peers].set(PSLOT)
    column = jax.random.randint(third, (), 0, N_SPACE)
    counts = counts.at[:, column].set(PSLOT)
    return counts.astype(jnp.int32)


def with_ends(drawn, stream_key, low, largest):
    longest = drawn.shape.index(max(drawn.shape))
    spots = []
    for shift in (0, 1):
        where = [jax.random.randint(jax.random.fold_in(stream_key, axis), (), 0, length) for axis, length in enumerate(drawn.shape)]
        where[longest] = (where[longest] + shift) % drawn.shape[longest]
        spots.append(tuple(where))
    return drawn.at[spots[0]].set(low).at[spots[1]].set(largest)


def level_of(key, shape, cuts, least, top_value):
    loudness, own = 1.0, jax.random.fold_in(key, 6)
    for position, blocks in cuts:
        draws = jnp.exp(jax.random.uniform(jax.random.fold_in(own, position), (blocks,), jnp.float32, least / len(cuts), top_value / len(cuts)))
        loudness = loudness * jnp.repeat(draws, shape[position] // blocks).reshape([-1 if axis == position else 1 for axis in range(len(shape))])
    return loudness


def gaussian(rng, extent, width, bound, cuts=(), kind=jnp.bfloat16):
    loudness = level_of(rng, extent, cuts, -0.22, 0.18) if cuts else 1.0
    array = jax.random.normal(rng, extent, jnp.float32) * width * loudness
    return jnp.minimum(jnp.maximum(array, -bound), bound).astype(kind)


def setup_inputs(seed: int = 0) -> dict:
    streams_of = jax.random.split(jax.random.key(seed), 16)
    adjoint_old = gaussian(streams_of[0], (INSTANCES, VARS, NI, NJ), 1.0, 6.0, ((0, 4), (2, 8)), jnp.float32)
    source_term = gaussian(streams_of[1], (INSTANCES, VARS, NI, NJ), 1.0, 6.0, ((0, 4), (2, 8)), jnp.float32)
    face_stream = jnp.clip(0.2 + 0.8 * jax.random.uniform(streams_of[2], (INSTANCES, NI, NJ), jnp.float32) ** level_of(streams_of[2], (INSTANCES, NI, NJ), ((0, 4), (1, 8)), -0.2, 0.2), 0.2, 1.0)
    face_pitch = jnp.clip(0.2 + 0.8 * jax.random.uniform(streams_of[3], (INSTANCES, NI, NJ), jnp.float32) ** level_of(streams_of[3], (INSTANCES, NI, NJ), ((0, 4), (1, 8)), -0.2, 0.2), 0.2, 1.0)
    diag_scale = jnp.clip(jnp.exp(math.log(0.4) - 1.3862944 * jax.random.uniform(streams_of[4], (INSTANCES, NI, NJ), jnp.float32) ** level_of(streams_of[4], (INSTANCES, NI, NJ), ((0, 4), (1, 8)), -0.2, 0.2)), 0.1, 0.4)
    volume = jnp.clip(jnp.exp(math.log(2.0) - 1.3862944 * jax.random.uniform(streams_of[5], (NI, NJ), jnp.float32) ** level_of(streams_of[5], (NI, NJ), ((0, 8),), -0.2, 0.2)), 0.5, 2.0)
    face_blocks = gaussian(streams_of[6], (4, VARS, VARS), VARS ** -0.5, 2.5, (), jnp.float32)
    diag_inverse = draw_diag_inverse(jax.random.fold_in(streams_of[15], 71), 0)
    periodic_block = gaussian(streams_of[8], (VARS, VARS), VARS ** -0.5, 2.5, (), jnp.float32)
    frequency = jnp.clip(jnp.exp(jax.random.uniform(streams_of[9], (1,), jnp.float32, math.log(0.5), math.log(2.0))), 0.5, 2.0)
    phase_shift = jax.random.randint(streams_of[10], (1,), 1, INSTANCES).astype(jnp.int32)
    periodic_cells = with_ends(jax.random.randint(streams_of[11], (N_SPACE, N_SPACE, PSLOT), 0, CI * NJ), jax.random.fold_in(streams_of[11], 1), 0, (CI * NJ) - 1).astype(jnp.int32)
    periodic_targets = with_ends(jax.random.randint(streams_of[12], (N_SPACE, N_SPACE, PSLOT), 0, CI * NJ), jax.random.fold_in(streams_of[12], 1), 0, (CI * NJ) - 1).astype(jnp.int32)
    periodic_weights = jnp.clip(0.5 + 1.0 * jax.random.uniform(streams_of[13], (N_SPACE, N_SPACE, PSLOT), jnp.float32) ** level_of(streams_of[13], (N_SPACE, N_SPACE, PSLOT), ((0, 8),), -0.2, 0.2), 0.5, 1.5)
    periodic_counts = draw_periodic_counts(jax.random.fold_in(streams_of[15], 71), 0)
    return dict(adjoint_old=adjoint_old, source_term=source_term, face_stream=face_stream, face_pitch=face_pitch, diag_scale=diag_scale, volume=volume, face_blocks=face_blocks, diag_inverse=diag_inverse, periodic_block=periodic_block, frequency=frequency, phase_shift=phase_shift, periodic_cells=periodic_cells, periodic_targets=periodic_targets, periodic_weights=periodic_weights, periodic_counts=periodic_counts)


def spectral_matrix():
    order = jnp.arange(INSTANCES, dtype=jnp.int32)
    offset = order[:, None] - order[None, :]
    parity = jnp.where(offset % 2 == 0, 1.0, -1.0)
    nonzero = offset != 0
    angle = math.pi * offset / INSTANCES
    safe = jnp.where(nonzero, angle, 1.0)
    return jnp.where(nonzero, 0.5 * parity * jnp.cos(safe) / jnp.sin(safe), 0.0).astype(jnp.float32)


def transposed(block, field):
    return jnp.einsum("vu,kvij->kuij", block, field, precision=lax.Precision.HIGHEST)


def neighbours(adjoint, face_stream, face_pitch, face_blocks):
    zero_row = jnp.zeros_like(adjoint[:, :, :1])
    weighted = face_stream[:, None] * adjoint
    from_lower = jnp.concatenate([zero_row, weighted[:, :, :-1]], axis=2)
    from_upper = face_stream[:, None] * jnp.concatenate([adjoint[:, :, 1:], zero_row], axis=2)
    zero_col = jnp.zeros_like(adjoint[..., :1])
    side = face_pitch[:, None] * adjoint
    from_left = jnp.concatenate([zero_col, side[..., :-1]], axis=3)
    from_right = face_pitch[:, None] * jnp.concatenate([adjoint[..., 1:], zero_col], axis=3)
    return (transposed(face_blocks[0], from_lower) + transposed(face_blocks[1], from_upper)
            + transposed(face_blocks[2], from_left) + transposed(face_blocks[3], from_right))


def reference(adjoint_old, source_term, face_stream, face_pitch, diag_scale, volume, face_blocks, diag_inverse,
              periodic_block, frequency, phase_shift, periodic_cells, periodic_targets, periodic_weights,
              periodic_counts):
    cells = CI * NJ
    flat = adjoint_old.reshape(INSTANCES, VARS, N_SPACE, cells)
    index = periodic_cells.reshape(N_SPACE, N_SPACE * PSLOT)
    picked = jnp.take_along_axis(flat, index[None, None], axis=3)
    slots = jnp.arange(PSLOT, dtype=jnp.int32)
    live = slots[None, None, :] < periodic_counts[:, :, None]
    weights = jnp.where(live, periodic_weights, 0.0).reshape(N_SPACE, N_SPACE * PSLOT)
    picked = jnp.einsum("vu,gvpr->gupr", periodic_block, picked, precision=lax.Precision.HIGHEST) * weights
    picked = jnp.roll(picked, phase_shift[0], axis=0)
    owner = jnp.arange(N_SPACE, dtype=jnp.int32)[None, :, None] * cells
    target = (owner + periodic_targets).reshape(-1)
    periodic = jnp.zeros((INSTANCES, VARS, N_SPACE * cells), adjoint_old.dtype)
    periodic = periodic.at[:, :, target].add(picked.reshape(INSTANCES, VARS, -1))
    periodic = periodic.reshape(INSTANCES, VARS, NI, NJ)
    dmat = spectral_matrix()
    adjoint = adjoint_old
    residual = adjoint_old
    for sweep_index in range(SWEEPS):
        coupling = frequency[0] * volume * jnp.einsum("mg,mvij->gvij", dmat, adjoint,
                                                      precision=lax.Precision.HIGHEST)
        residual = source_term - neighbours(adjoint, face_stream, face_pitch, face_blocks) - coupling - periodic
        adjoint = diag_scale[:, None] * jnp.einsum("guv,gvij->guij", diag_inverse, residual,
                                                   precision=lax.Precision.HIGHEST)
    return adjoint, residual
```

```python
import functools
import math

import jax
import jax.numpy as jnp
from jax import lax
from jax.experimental import pallas as pl
from jax.experimental.pallas import tpu as pltpu
from jax.sharding import PartitionSpec as P

SWEEPS = 2
TILE = 8
LANES = 128
WINDOW = 4
MESH = pl.DeviceIdType.MESH


def spectral_entry(offset, count):
    offset = offset % count
    if offset == 0 or 2 * offset == count:
        return 0.0
    return 0.5 * (-1.0) ** offset / math.tan(math.pi * offset / count)


def split_parts(value):
    parts = []
    for _ in range(3):
        part = value.astype(jnp.bfloat16)
        parts.append(part)
        value = value - part.astype(jnp.float32)
    return parts


def kernel(
    n_space,
    a_hbm,
    s_hbm,
    fs_hbm,
    fp_hbm,
    ds_hbm,
    vol_hbm,
    blocks,
    dinv,
    pblock,
    freq,
    shift,
    cells,
    targets,
    weights,
    counts,
    out_a,
    out_r,
    A,
    SP,
    R,
    FS,
    FP,
    DS,
    VOL,
    RX,
    SB,
    RL,
    COL,
    PICK,
    ALLP,
    ROUTED,
    ARR,
    load_sem,
    xs,
    xr,
    rs,
    rr,
    ss,
    sr,
    hs,
    hr,
    ps,
    pr,
    as_,
    ar,
    oa,
    orr,
):
    per_dev, variables, rows, width = a_hbm.shape
    instances = 4 * per_dev
    slots = cells.shape[2]
    nb = rows // TILE
    total = SWEEPS * nb
    inst = lax.axis_index("inst")
    me = lax.axis_index("space")
    odd = inst % 2
    sibling = inst + 1 - 2 * odd
    across = (inst + 2) % 4
    shift_bits = width.bit_length() - 1

    def local(src, dst, n):
        return pltpu.make_async_copy(src, dst, load_sem.at[n])

    inner = pl.ds(TILE, rows)
    loads = [
        local(a_hbm, A.at[0, :, :, inner, :], 0),
        local(fs_hbm, FS.at[:, inner, :], 1),
        local(s_hbm, SP, 2),
        local(fp_hbm, FP, 3),
        local(ds_hbm, DS, 4),
        local(vol_hbm, VOL, 5),
    ]
    for copy in loads:
        copy.start()

    barrier = pltpu.get_barrier_semaphore()
    pl.semaphore_signal(barrier, inc=1, device_id={"inst": sibling}, device_id_type=MESH)
    pl.semaphore_signal(barrier, inc=1, device_id={"inst": across}, device_id_type=MESH)

    @pl.loop(1, n_space)
    def _(j):
        pl.semaphore_signal(
            barrier, inc=1, device_id={"space": (me + j) % n_space}, device_id_type=MESH
        )

    def remote(src, dst, send, recv, **device):
        return pltpu.make_async_remote_copy(
            src_ref=src, dst_ref=dst, send_sem=send, recv_sem=recv, device_id=device,
            device_id_type=MESH,
        )

    def place(t):
        sweep = t // nb
        block = (t % nb + nb - 1) % nb
        return sweep, block, pl.multiple_of(block * TILE, TILE)

    def x_copy(t):
        sweep, _, row = place(t)
        return remote(
            A.at[sweep, :, :, pl.ds(row + TILE, TILE), :],
            RX.at[sweep, :, :, pl.ds(row, TILE), :],
            xs.at[t], xr.at[t], inst=across,
        )

    def sib_copy(t):
        sweep, _, row = place(t)
        return remote(
            A.at[sweep, :, :, pl.ds(row + TILE, TILE), :],
            SB.at[sweep, :, :, pl.ds(row, TILE), :],
            ss.at[t], sr.at[t], inst=sibling,
        )

    def relay_copy(t):
        sweep, _, row = place(t)
        here = RX.at[sweep, :, :, pl.ds(row, TILE), :]
        return remote(
            here, RL.at[sweep, :, :, pl.ds(row, TILE), :], rs.at[t], rr.at[t], inst=sibling
        )

    has_above = me < n_space - 1
    has_below = me > 0
    above = (me + 1) % n_space
    below = (me + n_space - 1) % n_space

    def halo_up(sweep):
        return remote(
            A.at[sweep, :, :, pl.ds(rows, TILE), :],
            A.at[sweep, :, :, pl.ds(0, TILE), :],
            hs.at[2 * sweep], hr.at[2 * sweep], space=above,
        )

    def halo_down(sweep):
        return remote(
            A.at[sweep, :, :, pl.ds(TILE, TILE), :],
            A.at[sweep, :, :, pl.ds(rows + TILE, TILE), :],
            hs.at[2 * sweep + 1], hr.at[2 * sweep + 1], space=below,
        )

    def halo_face():
        last = 2 * SWEEPS
        return remote(
            FS.at[:, pl.ds(rows, TILE), :], FS.at[:, pl.ds(0, TILE), :],
            hs.at[last], hr.at[last], space=above,
        )

    @pl.when(me == 0)
    def _():
        FS[:, 0:TILE, :] = jnp.zeros((per_dev, TILE, width), jnp.float32)
        for sweep in range(SWEEPS):
            A[sweep, :, :, 0:TILE, :] = jnp.zeros((per_dev, variables, TILE, width), jnp.float32)

    @pl.when(me == n_space - 1)
    def _():
        for sweep in range(SWEEPS):
            A[sweep, :, :, rows + TILE : rows + 2 * TILE, :] = jnp.zeros(
                (per_dev, variables, TILE, width), jnp.float32
            )

    loads[0].wait()
    pl.semaphore_wait(barrier, n_space + 1)
    for t in range(WINDOW):
        x_copy(t).start()
    loads[1].wait()

    @pl.when(has_above)
    def _():
        halo_up(0).start()
        halo_face().start()

    @pl.when(has_below)
    def _():
        halo_down(0).start()

    @pl.loop(0, nb)
    def _(t):
        sib_copy(t).start()

    sub_w = lax.broadcasted_iota(jnp.int32, (width, slots), 0)
    sub_r = lax.broadcasted_iota(jnp.int32, (rows, slots), 0)

    def column_table(index, chunk):
        for q in range(TILE):
            line = index(chunk * TILE + q)
            column = jnp.bitwise_and(line, width - 1)
            hot = jnp.where(sub_w == column, 1.0, 0.0).astype(jnp.bfloat16)
            COL[:, q * slots : (q + 1) * slots] = hot

    def cell_line(q):
        return cells[0, pl.ds(q, 1), :]

    def target_line(p):
        return targets[p, 0:1, :]

    chunks = n_space // TILE

    @pl.loop(0, chunks)
    def _(chunk):
        column_table(cell_line, chunk)

        @pl.loop(0, per_dev)
        def _(k):
            field = A[0, k, :, TILE : TILE + rows, :].reshape(variables * rows, width)
            found = None
            for part in split_parts(field):
                term = jnp.dot(part, COL[...], preferred_element_type=jnp.float32)
                found = term if found is None else found + term
            for q in range(TILE):
                hit = sub_r == lax.shift_right_logical(cell_line(chunk * TILE + q), shift_bits)
                for v in range(variables):
                    piece = found[v * rows : (v + 1) * rows, q * slots : (q + 1) * slots]
                    PICK[k, v, chunk, q : q + 1, :] = jnp.sum(
                        jnp.where(hit, piece, 0.0), axis=0, keepdims=True
                    )

        lane = lax.broadcasted_iota(jnp.int32, (TILE, slots), 1)
        sub = lax.broadcasted_iota(jnp.int32, (TILE, slots), 0)
        limit = jnp.zeros((TILE, slots), jnp.int32)
        for q in range(TILE):
            limit = jnp.where(sub == q, counts[0, chunk * TILE + q], limit)
        first = pl.multiple_of(chunk * TILE, TILE)
        weight = jnp.where(lane < limit, weights[0, pl.ds(first, TILE), :], 0.0)

        for k in range(per_dev):
            picked = [PICK[k, v, chunk] for v in range(variables)]
            for u in range(variables):
                mixed = pblock[0, u] * picked[0]
                for v in range(1, variables):
                    mixed = mixed + pblock[v, u] * picked[v]
                ALLP[0, k, u, chunk] = mixed * weight

    p_x = remote(ALLP.at[0], ALLP.at[2], ps.at[0], pr.at[0], inst=across)
    p_sib = remote(ALLP.at[0], ALLP.at[3 - 2 * odd], ps.at[1], pr.at[1 + odd], inst=sibling)
    p_rel = remote(ALLP.at[2], ALLP.at[1 + 2 * odd], ps.at[2], pr.at[2 - odd], inst=sibling)
    p_sib_in = remote(ALLP.at[0], ALLP.at[1 + 2 * odd], ps.at[1], pr.at[2 - odd], inst=sibling)
    p_rel_in = remote(ALLP.at[2], ALLP.at[3 - 2 * odd], ps.at[2], pr.at[1 + odd], inst=sibling)
    p_x.start()
    p_sib.start()
    p_x.wait_recv()
    p_rel.start()
    p_sib_in.wait_recv()
    p_rel_in.wait_recv()
    for k in range(per_dev):
        wanted = lax.rem(k - shift[0] + 2 * instances, instances)
        group = lax.div(wanted, per_dev)
        member = lax.rem(wanted, per_dev)

        @pl.loop(0, chunks)
        def _(chunk):
            for u in range(variables):
                value = ALLP[group, member, u, chunk]
                for q in range(TILE):
                    ROUTED[chunk * TILE + q, k * variables + u : k * variables + u + 1, :] = value[
                        q : q + 1, :
                    ]

    def a2a(j):
        return remote(
            ROUTED.at[(me + j) % n_space], ARR.at[me], as_.at[j], ar.at[j],
            space=(me + j) % n_space,
        )

    @pl.loop(1, n_space)
    def _(j):
        a2a(j).start()

    ARR[me] = ROUTED[me]
    loads[2].wait()
    column_table(target_line, 0)

    @pl.loop(1, n_space)
    def _(j):
        remote(
            ROUTED.at[0], ARR.at[(me + n_space - j) % n_space], as_.at[j], ar.at[j],
            space=(me + j) % n_space,
        ).wait_recv()

    @pl.loop(0, chunks)
    def _(chunk):
        if chunks > 1:
            column_table(target_line, chunk)

        for k in range(per_dev):
            arrived = [
                split_parts(ARR[chunk * TILE + p, k * variables : (k + 1) * variables, :])
                for p in range(TILE)
            ]
            hits = [
                sub_r == lax.shift_right_logical(target_line(chunk * TILE + p), shift_bits)
                for p in range(TILE)
            ]
            for u in range(variables):
                total_u = None
                for part in range(3):
                    spread = jnp.concatenate(
                        [
                            jnp.where(
                                hits[p], arrived[p][part][u : u + 1, :].astype(jnp.float32), 0.0
                            ).astype(jnp.bfloat16)
                            for p in range(TILE)
                        ],
                        axis=1,
                    )
                    term = lax.dot_general(
                        spread, COL[...], (((1,), (1,)), ((), ())),
                        preferred_element_type=jnp.float32,
                    )
                    total_u = term if total_u is None else total_u + term
                SP[k, u] = SP[k, u] - total_u

    for copy in loads[3:]:
        copy.wait()

    @pl.when(has_below)
    def _():
        halo_up(0).wait_recv()
        halo_face().wait_recv()

    @pl.when(has_above)
    def _():
        halo_down(0).wait_recv()

    d1, d2, d3 = (spectral_entry(d, instances) for d in (1, 2, 3))
    is_odd = odd == 1

    def pick(even_value, odd_value):
        return jnp.where(is_odd, jnp.float32(odd_value), jnp.float32(even_value))

    nxt = ((d2, d3), (d1, d2))
    prv = ((-d2, -d1), (-d3, -d2))
    c_sib = [[pick(nxt[g][m], prv[g][m]) for m in range(2)] for g in range(2)]
    c_rel = [[pick(prv[g][m], nxt[g][m]) for m in range(2)] for g in range(2)]
    c_own = (d1, -d1)
    c_x = (-d3, d3)

    sub8 = lax.broadcasted_iota(jnp.int32, (TILE, width), 0)
    lane8 = lax.broadcasted_iota(jnp.int32, (TILE, width), 1)

    @pl.loop(0, total)
    def _(t):
        sweep, block, row = place(t)
        here = pl.ds(row, TILE)
        mid = pl.ds(row + TILE, TILE)
        low = pl.ds(row, TILE)
        high = pl.ds(row + 2 * TILE, TILE)

        x_copy(t).wait()

        @pl.when(t + WINDOW < total)
        def _():
            x_copy(t + WINDOW).start()

        relay_copy(t).start()

        @pl.when(t == nb)
        def _():
            @pl.when(has_below)
            def _():
                halo_up(1).wait_recv()

            @pl.when(has_above)
            def _():
                halo_down(1).wait_recv()

        sib_copy(t).wait_recv()
        relay_copy(t).wait_recv()
        scaled = freq[0] * VOL[here, :]

        for k in range(per_dev):
            other = 1 - k
            acc = []
            for u in range(variables):
                s = c_own[k] * A[sweep, other, u, mid, :] + c_x[k] * RX[sweep, other, u, here, :]
                for m in range(2):
                    s = s + c_sib[k][m] * SB[sweep, m, u, here, :]
                    s = s + c_rel[k][m] * RL[sweep, m, u, here, :]
                acc.append(SP[k, u, here, :] - scaled * s)
            fs_low = jnp.where(sub8 == TILE - 1, FS[k, low, :], FS[k, mid, :])
            fs_mid = FS[k, mid, :]
            fp = jnp.where(lane8 == width - 1, 0.0, FP[k, here, :])
            for v in range(variables):
                a = A[sweep, k, v, mid, :]
                x = pltpu.roll(
                    fs_low * jnp.where(sub8 == TILE - 1, A[sweep, k, v, low, :], a), 1, 0
                )
                y = fs_mid * pltpu.roll(
                    jnp.where(sub8 == 0, A[sweep, k, v, high, :], a), TILE - 1, 0
                )
                left = pltpu.roll(fp * a, 1, 1)
                right = fp * pltpu.roll(a, width - 1, 1)
                for u in range(variables):
                    acc[u] = acc[u] - (
                        (blocks[0, v, u] * x + blocks[1, v, u] * y)
                        + (blocks[2, v, u] * left + blocks[3, v, u] * right)
                    )
            scale = DS[k, here, :]
            for u in range(variables):
                R[k, u, here, :] = acc[u]
            for u in range(variables):
                new = dinv[k, u, 0] * acc[0]
                for v in range(1, variables):
                    new = new + dinv[k, u, v] * acc[v]
                A[sweep + 1, k, u, mid, :] = scale * new

        @pl.when(sweep == 0)
        def _():
            sib_copy(t + nb).start()

        @pl.when(t == 1)
        def _():
            @pl.when(has_above)
            def _():
                halo_up(1).start()

            @pl.when(has_below)
            def _():
                halo_down(1).start()

        @pl.when(sweep == SWEEPS - 1)
        def _():
            pltpu.make_async_copy(
                A.at[SWEEPS, :, :, mid, :], out_a.at[:, :, here, :], oa.at[block]
            ).start()
            pltpu.make_async_copy(
                R.at[:, :, here, :], out_r.at[:, :, here, :], orr.at[block]
            ).start()

    @pl.loop(0, total)
    def _(t):
        relay_copy(t).wait_send()
        sib_copy(t).wait_send()

    p_x.wait_send()
    p_sib.wait_send()
    p_rel.wait_send()

    @pl.loop(1, n_space)
    def _(j):
        a2a(j).wait_send()

    @pl.when(has_above)
    def _():
        for sweep in range(SWEEPS):
            halo_up(sweep).wait_send()
        halo_face().wait_send()

    @pl.when(has_below)
    def _():
        for sweep in range(SWEEPS):
            halo_down(sweep).wait_send()

    @pl.loop(0, nb)
    def _(b):
        here = pl.ds(pl.multiple_of(b * TILE, TILE), TILE)
        mid = pl.ds(pl.multiple_of(b * TILE, TILE) + TILE, TILE)
        pltpu.make_async_copy(
            A.at[SWEEPS, :, :, mid, :], out_a.at[:, :, here, :], oa.at[b]
        ).wait()
        pltpu.make_async_copy(R.at[:, :, here, :], out_r.at[:, :, here, :], orr.at[b]).wait()


def body(n_space, *args):
    per_dev, variables, rows, width = args[0].shape
    slots = args[11].shape[2]
    nb = rows // TILE
    chunks = n_space // TILE
    total = SWEEPS * nb
    f32 = jnp.float32
    hbm = pl.BlockSpec(memory_space=pl.ANY)
    smem = pl.BlockSpec(memory_space=pltpu.SMEM)
    vmem = pl.BlockSpec(memory_space=pltpu.VMEM)
    dma = pltpu.SemaphoreType.DMA
    field = (per_dev, variables, rows, width)
    out = jax.ShapeDtypeStruct(field, f32)
    return pl.pallas_call(
        functools.partial(kernel, n_space),
        out_shape=(out, out),
        in_specs=[hbm] * 6 + [smem] * 5 + [vmem] * 3 + [smem],
        out_specs=(hbm, hbm),
        scratch_shapes=[
            pltpu.VMEM((SWEEPS + 1, per_dev, variables, rows + 2 * TILE, width), f32),
            pltpu.VMEM(field, f32),
            pltpu.VMEM(field, f32),
            pltpu.VMEM((per_dev, rows + TILE, width), f32),
            pltpu.VMEM((per_dev, rows, width), f32),
            pltpu.VMEM((per_dev, rows, width), f32),
            pltpu.VMEM((rows, width), f32),
            pltpu.VMEM((SWEEPS,) + field, f32),
            pltpu.VMEM((SWEEPS,) + field, f32),
            pltpu.VMEM((SWEEPS,) + field, f32),
            pltpu.VMEM((width, TILE * slots), jnp.bfloat16),
            pltpu.VMEM((per_dev, variables, chunks, TILE, slots), f32),
            pltpu.VMEM((4, per_dev, variables, chunks, TILE, slots), f32),
            pltpu.VMEM((n_space, per_dev * variables, slots), f32),
            pltpu.VMEM((n_space, per_dev * variables, slots), f32),
            dma((6,)),
            dma((total,)),
            dma((total,)),
            dma((total,)),
            dma((total,)),
            dma((total,)),
            dma((total,)),
            dma((2 * SWEEPS + 1,)),
            dma((2 * SWEEPS + 1,)),
            dma((3,)),
            dma((3,)),
            dma((n_space,)),
            dma((n_space,)),
            dma((nb,)),
            dma((nb,)),
        ],
        compiler_params=pltpu.CompilerParams(
            collective_id=0, has_side_effects=True, vmem_limit_bytes=56 * 1024 * 1024
        ),
    )(*args)


def solution(mesh):
    in_specs = (
        P("inst", None, "space", None),
        P("inst", None, "space", None),
        P("inst", "space", None),
        P("inst", "space", None),
        P("inst", "space", None),
        P("space", None),
        P(),
        P("inst", None, None),
        P(),
        P(),
        P(),
        P("space", None, None),
        P(None, "space", None),
        P("space", None, None),
        P("space", None),
    )
    out_specs = (P("inst", None, "space", None), P("inst", None, "space", None))
    return jax.shard_map(
        functools.partial(body, mesh.shape["space"]),
        mesh=mesh,
        in_specs=in_specs,
        out_specs=out_specs,
        check_vma=False,
    )
```

```python
import functools
import math

import jax
import jax.numpy as jnp
from jax import lax
from jax.experimental import pallas as pl
from jax.experimental.pallas import tpu as pltpu
from jax.sharding import PartitionSpec as P

SWEEPS = 2
TILE = 8
LANES = 128
WINDOW = 3
PARTS = 2
MESH = pl.DeviceIdType.MESH


def spectral_entry(offset, count):
    offset = offset % count
    if offset == 0 or 2 * offset == count:
        return 0.0
    return 0.5 * (-1.0) ** offset / math.tan(math.pi * offset / count)


def split_parts(value):
    parts = []
    for _ in range(PARTS):
        part = value.astype(jnp.bfloat16)
        parts.append(part)
        value = value - part.astype(jnp.float32)
    return parts


def kernel(
    n_space,
    a_hbm,
    s_hbm,
    fs_hbm,
    fp_hbm,
    ds_hbm,
    vol_hbm,
    blocks,
    dinv,
    pblock,
    freq,
    shift,
    cells,
    targets,
    weights,
    counts,
    out_a,
    out_r,
    A,
    SP,
    R,
    FS,
    FP,
    DS,
    VOL,
    RX,
    SB,
    RL,
    COL,
    PICK,
    ALLP,
    ROUTED,
    ARR,
    LHS,
    load_sem,
    xs,
    xr,
    rs,
    rr,
    ss,
    sr,
    hs,
    hr,
    ps,
    pr,
    as_,
    ar,
    oa,
    orr,
):
    per_dev, variables, rows, width = a_hbm.shape
    instances = 4 * per_dev
    slots = cells.shape[2]
    nb = rows // TILE
    total = SWEEPS * nb
    inst = lax.axis_index("inst")
    me = lax.axis_index("space")
    odd = inst % 2
    sibling = inst + 1 - 2 * odd
    across = (inst + 2) % 4
    shift_bits = width.bit_length() - 1

    def local(src, dst, n):
        return pltpu.make_async_copy(src, dst, load_sem.at[n])

    inner = pl.ds(TILE, rows)
    loads = [
        local(a_hbm, A.at[0, :, :, inner, :], 0),
        local(fs_hbm, FS.at[:, inner, :], 1),
        local(s_hbm, SP, 2),
        local(fp_hbm, FP, 3),
        local(ds_hbm, DS, 4),
        local(vol_hbm, VOL, 5),
    ]
    for copy in loads:
        copy.start()

    barrier = pltpu.get_barrier_semaphore()
    pl.semaphore_signal(barrier, inc=1, device_id={"inst": sibling}, device_id_type=MESH)
    pl.semaphore_signal(barrier, inc=1, device_id={"inst": across}, device_id_type=MESH)

    @pl.loop(1, n_space)
    def _(j):
        pl.semaphore_signal(
            barrier, inc=1, device_id={"space": (me + j) % n_space}, device_id_type=MESH
        )

    def remote(src, dst, send, recv, **device):
        return pltpu.make_async_remote_copy(
            src_ref=src, dst_ref=dst, send_sem=send, recv_sem=recv, device_id=device,
            device_id_type=MESH,
        )

    def place(t):
        sweep = t // nb
        block = (t % nb + nb - 1) % nb
        return sweep, block, pl.multiple_of(block * TILE, TILE)

    def x_copy(t):
        sweep, _, row = place(t)
        return remote(
            A.at[sweep, :, :, pl.ds(row + TILE, TILE), :],
            RX.at[sweep, :, :, pl.ds(row, TILE), :],
            xs.at[t], xr.at[t], inst=across,
        )

    def sib_copy(t):
        sweep, _, row = place(t)
        return remote(
            A.at[sweep, :, :, pl.ds(row + TILE, TILE), :],
            SB.at[sweep, :, :, pl.ds(row, TILE), :],
            ss.at[t], sr.at[t], inst=sibling,
        )

    def relay_copy(t):
        sweep, _, row = place(t)
        here = RX.at[sweep, :, :, pl.ds(row, TILE), :]
        return remote(
            here, RL.at[sweep, :, :, pl.ds(row, TILE), :], rs.at[t], rr.at[t], inst=sibling
        )

    def forward(t):
        x_copy(t).wait()
        relay_copy(t).start()

    has_above = me < n_space - 1
    has_below = me > 0
    above = (me + 1) % n_space
    below = (me + n_space - 1) % n_space

    def halo_up(sweep):
        return remote(
            A.at[sweep, :, :, pl.ds(rows, TILE), :],
            A.at[sweep, :, :, pl.ds(0, TILE), :],
            hs.at[2 * sweep], hr.at[2 * sweep], space=above,
        )

    def halo_down(sweep):
        return remote(
            A.at[sweep, :, :, pl.ds(TILE, TILE), :],
            A.at[sweep, :, :, pl.ds(rows + TILE, TILE), :],
            hs.at[2 * sweep + 1], hr.at[2 * sweep + 1], space=below,
        )

    def halo_face():
        last = 2 * SWEEPS
        return remote(
            FS.at[:, pl.ds(rows, TILE), :], FS.at[:, pl.ds(0, TILE), :],
            hs.at[last], hr.at[last], space=above,
        )

    @pl.when(me == 0)
    def _():
        FS[:, 0:TILE, :] = jnp.zeros((per_dev, TILE, width), jnp.float32)
        for sweep in range(SWEEPS):
            A[sweep, :, :, 0:TILE, :] = jnp.zeros((per_dev, variables, TILE, width), jnp.float32)

    @pl.when(me == n_space - 1)
    def _():
        for sweep in range(SWEEPS):
            A[sweep, :, :, rows + TILE : rows + 2 * TILE, :] = jnp.zeros(
                (per_dev, variables, TILE, width), jnp.float32
            )

    loads[0].wait()
    pl.semaphore_wait(barrier, n_space + 1)

    @pl.loop(0, nb)
    def _(t):
        x_copy(t).start()

    loads[1].wait()

    @pl.when(has_above)
    def _():
        halo_up(0).start()
        halo_face().start()

    @pl.when(has_below)
    def _():
        halo_down(0).start()

    @pl.loop(0, nb)
    def _(t):
        sib_copy(t).start()

    sub_w = lax.broadcasted_iota(jnp.int32, (width, slots), 0)
    sub_r = lax.broadcasted_iota(jnp.int32, (rows, slots), 0)

    def column_table(index, chunk):
        for q in range(TILE):
            line = index(chunk * TILE + q)
            column = jnp.bitwise_and(line, width - 1)
            hot = jnp.where(sub_w == column, 1.0, 0.0).astype(jnp.bfloat16)
            COL[:, q * slots : (q + 1) * slots] = hot

    def cell_line(q):
        return cells[0, pl.ds(q, 1), :]

    def target_line(p):
        return targets[p, 0:1, :]

    chunks = n_space // TILE

    @pl.loop(0, chunks)
    def _(chunk):
        column_table(cell_line, chunk)

        @pl.loop(0, per_dev)
        def _(k):
            field = A[0, k, :, TILE : TILE + rows, :].reshape(variables * rows, width)
            stacked = jnp.concatenate(split_parts(field), axis=0)
            terms = jnp.dot(stacked, COL[...], preferred_element_type=jnp.float32)
            height = variables * rows
            found = terms[:height]
            for part in range(1, PARTS):
                found = found + terms[part * height : (part + 1) * height]
            for q in range(TILE):
                hit = sub_r == lax.shift_right_logical(cell_line(chunk * TILE + q), shift_bits)
                for v in range(variables):
                    piece = found[v * rows : (v + 1) * rows, q * slots : (q + 1) * slots]
                    PICK[k, v, chunk, q : q + 1, :] = jnp.sum(
                        jnp.where(hit, piece, 0.0), axis=0, keepdims=True
                    )

        lane = lax.broadcasted_iota(jnp.int32, (TILE, slots), 1)
        sub = lax.broadcasted_iota(jnp.int32, (TILE, slots), 0)
        limit = jnp.zeros((TILE, slots), jnp.int32)
        for q in range(TILE):
            limit = jnp.where(sub == q, counts[0, chunk * TILE + q], limit)
        first = pl.multiple_of(chunk * TILE, TILE)
        weight = jnp.where(lane < limit, weights[0, pl.ds(first, TILE), :], 0.0)

        for k in range(per_dev):
            picked = [PICK[k, v, chunk] for v in range(variables)]
            for u in range(variables):
                mixed = pblock[0, u] * picked[0]
                for v in range(1, variables):
                    mixed = mixed + pblock[v, u] * picked[v]
                ALLP[0, k, u, chunk] = mixed * weight

    p_x = remote(ALLP.at[0], ALLP.at[2], ps.at[0], pr.at[0], inst=across)
    p_sib = remote(ALLP.at[0], ALLP.at[3 - 2 * odd], ps.at[1], pr.at[1 + odd], inst=sibling)
    p_rel = remote(ALLP.at[2], ALLP.at[1 + 2 * odd], ps.at[2], pr.at[2 - odd], inst=sibling)
    p_sib_in = remote(ALLP.at[0], ALLP.at[1 + 2 * odd], ps.at[1], pr.at[2 - odd], inst=sibling)
    p_rel_in = remote(ALLP.at[2], ALLP.at[3 - 2 * odd], ps.at[2], pr.at[1 + odd], inst=sibling)
    p_x.start()
    p_sib.start()
    forward(0)
    p_x.wait_recv()
    p_rel.start()
    p_sib_in.wait_recv()
    p_rel_in.wait_recv()
    for k in range(per_dev):
        wanted = lax.rem(k - shift[0] + 2 * instances, instances)
        group = lax.div(wanted, per_dev)
        member = lax.rem(wanted, per_dev)

        @pl.loop(0, chunks)
        def _(chunk):
            for u in range(variables):
                value = ALLP[group, member, u, chunk]
                for q in range(TILE):
                    ROUTED[chunk * TILE + q, k, u : u + 1, :] = value[q : q + 1, :]

    def a2a(j):
        return remote(
            ROUTED.at[(me + j) % n_space], ARR.at[me], as_.at[j], ar.at[j],
            space=(me + j) % n_space,
        )

    @pl.loop(1, n_space)
    def _(j):
        a2a(j).start()

    ARR[me] = ROUTED[me]
    forward(1)
    loads[2].wait()
    column_table(target_line, 0)

    @pl.loop(1, n_space)
    def _(j):
        remote(
            ROUTED.at[0], ARR.at[(me + n_space - j) % n_space], as_.at[j], ar.at[j],
            space=(me + j) % n_space,
        ).wait_recv()

    @pl.loop(0, chunks)
    def _(chunk):
        if chunks > 1:
            column_table(target_line, chunk)

        for k in range(per_dev):
            for p in range(TILE):
                hit = sub_r == lax.shift_right_logical(target_line(chunk * TILE + p), shift_bits)
                parts = split_parts(ARR[chunk * TILE + p, k])
                for n, part in enumerate(parts):
                    for u in range(variables):
                        start = (n * variables + u) * rows
                        LHS[start : start + rows, p * slots : (p + 1) * slots] = jnp.where(
                            hit, part[u : u + 1, :].astype(jnp.float32), 0.0
                        ).astype(jnp.bfloat16)
            terms = lax.dot_general(
                LHS[...], COL[...], (((1,), (1,)), ((), ())), preferred_element_type=jnp.float32
            )
            height = variables * rows
            summed = terms[:height]
            for part in range(1, PARTS):
                summed = summed + terms[part * height : (part + 1) * height]
            SP[k] = SP[k] - summed.reshape(variables, rows, width)

    @pl.loop(2, nb - 2)
    def _(t):
        forward(t)

    for copy in loads[3:]:
        copy.wait()

    @pl.when(has_below)
    def _():
        halo_up(0).wait_recv()
        halo_face().wait_recv()

    @pl.when(has_above)
    def _():
        halo_down(0).wait_recv()

    d1, d2, d3 = (spectral_entry(d, instances) for d in (1, 2, 3))
    is_odd = odd == 1

    def pick(even_value, odd_value):
        return jnp.where(is_odd, jnp.float32(odd_value), jnp.float32(even_value))

    nxt = ((d2, d3), (d1, d2))
    prv = ((-d2, -d1), (-d3, -d2))
    c_sib = [[pick(nxt[g][m], prv[g][m]) for m in range(2)] for g in range(2)]
    c_rel = [[pick(prv[g][m], nxt[g][m]) for m in range(2)] for g in range(2)]
    c_own = (d1, -d1)
    c_x = (-d3, d3)

    sub8 = lax.broadcasted_iota(jnp.int32, (TILE, width), 0)
    lane8 = lax.broadcasted_iota(jnp.int32, (TILE, width), 1)

    @pl.loop(0, total)
    def _(t):
        sweep, block, row = place(t)
        here = pl.ds(row, TILE)
        mid = pl.ds(row + TILE, TILE)
        low = pl.ds(row, TILE)
        high = pl.ds(row + 2 * TILE, TILE)

        @pl.when(t < 2)
        def _():
            forward(t + nb - 2)

        @pl.when(t == nb)
        def _():
            forward(t)

        @pl.when((t >= nb) & (t + WINDOW < total))
        def _():
            x_copy(t + WINDOW).start()

        @pl.when((t >= nb) & (t + 1 < total))
        def _():
            forward(t + 1)

        @pl.when(t == nb)
        def _():
            @pl.when(has_below)
            def _():
                halo_up(1).wait_recv()

            @pl.when(has_above)
            def _():
                halo_down(1).wait_recv()

        sib_copy(t).wait_recv()
        relay_copy(t).wait_recv()
        scaled = freq[0] * VOL[here, :]

        for k in range(per_dev):
            other = 1 - k
            acc = []
            for u in range(variables):
                s = c_own[k] * A[sweep, other, u, mid, :] + c_x[k] * RX[sweep, other, u, here, :]
                for m in range(2):
                    s = s + c_sib[k][m] * SB[sweep, m, u, here, :]
                    s = s + c_rel[k][m] * RL[sweep, m, u, here, :]
                acc.append(SP[k, u, here, :] - scaled * s)
            fs_low = jnp.where(sub8 == TILE - 1, FS[k, low, :], FS[k, mid, :])
            fs_mid = FS[k, mid, :]
            fp = jnp.where(lane8 == width - 1, 0.0, FP[k, here, :])
            for v in range(variables):
                a = A[sweep, k, v, mid, :]
                x = pltpu.roll(
                    fs_low * jnp.where(sub8 == TILE - 1, A[sweep, k, v, low, :], a), 1, 0
                )
                y = fs_mid * pltpu.roll(
                    jnp.where(sub8 == 0, A[sweep, k, v, high, :], a), TILE - 1, 0
                )
                left = pltpu.roll(fp * a, 1, 1)
                right = fp * pltpu.roll(a, width - 1, 1)
                for u in range(variables):
                    acc[u] = acc[u] - (
                        (blocks[0, v, u] * x + blocks[1, v, u] * y)
                        + (blocks[2, v, u] * left + blocks[3, v, u] * right)
                    )
            scale = DS[k, here, :]
            for u in range(variables):
                R[k, u, here, :] = acc[u]
            for u in range(variables):
                new = dinv[k, u, 0] * acc[0]
                for v in range(1, variables):
                    new = new + dinv[k, u, v] * acc[v]
                A[sweep + 1, k, u, mid, :] = scale * new

        @pl.when(sweep == 0)
        def _():
            sib_copy(t + nb).start()

            @pl.when(t < WINDOW)
            def _():
                x_copy(t + nb).start()

        @pl.when(t == 1)
        def _():
            @pl.when(has_above)
            def _():
                halo_up(1).start()

            @pl.when(has_below)
            def _():
                halo_down(1).start()

        @pl.when(sweep == SWEEPS - 1)
        def _():
            pltpu.make_async_copy(
                A.at[SWEEPS, :, :, mid, :], out_a.at[:, :, here, :], oa.at[block]
            ).start()
            pltpu.make_async_copy(
                R.at[:, :, here, :], out_r.at[:, :, here, :], orr.at[block]
            ).start()

    @pl.loop(0, total)
    def _(t):
        relay_copy(t).wait_send()
        sib_copy(t).wait_send()

    p_x.wait_send()
    p_sib.wait_send()
    p_rel.wait_send()

    @pl.loop(1, n_space)
    def _(j):
        a2a(j).wait_send()

    @pl.when(has_above)
    def _():
        for sweep in range(SWEEPS):
            halo_up(sweep).wait_send()
        halo_face().wait_send()

    @pl.when(has_below)
    def _():
        for sweep in range(SWEEPS):
            halo_down(sweep).wait_send()

    @pl.loop(0, nb)
    def _(b):
        here = pl.ds(pl.multiple_of(b * TILE, TILE), TILE)
        mid = pl.ds(pl.multiple_of(b * TILE, TILE) + TILE, TILE)
        pltpu.make_async_copy(
            A.at[SWEEPS, :, :, mid, :], out_a.at[:, :, here, :], oa.at[b]
        ).wait()
        pltpu.make_async_copy(R.at[:, :, here, :], out_r.at[:, :, here, :], orr.at[b]).wait()


def body(n_space, *args):
    per_dev, variables, rows, width = args[0].shape
    slots = args[11].shape[2]
    nb = rows // TILE
    chunks = n_space // TILE
    total = SWEEPS * nb
    f32 = jnp.float32
    hbm = pl.BlockSpec(memory_space=pl.ANY)
    smem = pl.BlockSpec(memory_space=pltpu.SMEM)
    vmem = pl.BlockSpec(memory_space=pltpu.VMEM)
    dma = pltpu.SemaphoreType.DMA
    field = (per_dev, variables, rows, width)
    out = jax.ShapeDtypeStruct(field, f32)
    return pl.pallas_call(
        functools.partial(kernel, n_space),
        out_shape=(out, out),
        in_specs=[hbm] * 6 + [smem] * 5 + [vmem] * 3 + [smem],
        out_specs=(hbm, hbm),
        scratch_shapes=[
            pltpu.VMEM((SWEEPS + 1, per_dev, variables, rows + 2 * TILE, width), f32),
            pltpu.VMEM(field, f32),
            pltpu.VMEM(field, f32),
            pltpu.VMEM((per_dev, rows + TILE, width), f32),
            pltpu.VMEM((per_dev, rows, width), f32),
            pltpu.VMEM((per_dev, rows, width), f32),
            pltpu.VMEM((rows, width), f32),
            pltpu.VMEM((SWEEPS,) + field, f32),
            pltpu.VMEM((SWEEPS,) + field, f32),
            pltpu.VMEM((SWEEPS,) + field, f32),
            pltpu.VMEM((width, TILE * slots), jnp.bfloat16),
            pltpu.VMEM((per_dev, variables, chunks, TILE, slots), f32),
            pltpu.VMEM((4, per_dev, variables, chunks, TILE, slots), f32),
            pltpu.VMEM((n_space, per_dev, variables, slots), f32),
            pltpu.VMEM((n_space, per_dev, variables, slots), f32),
            pltpu.VMEM((PARTS * variables * rows, TILE * slots), jnp.bfloat16),
            dma((6,)),
            dma((total,)),
            dma((total,)),
            dma((total,)),
            dma((total,)),
            dma((total,)),
            dma((total,)),
            dma((2 * SWEEPS + 1,)),
            dma((2 * SWEEPS + 1,)),
            dma((3,)),
            dma((3,)),
            dma((n_space,)),
            dma((n_space,)),
            dma((nb,)),
            dma((nb,)),
        ],
        compiler_params=pltpu.CompilerParams(
            collective_id=0, has_side_effects=True, vmem_limit_bytes=56 * 1024 * 1024
        ),
    )(*args)


def solution(mesh):
    in_specs = (
        P("inst", None, "space", None),
        P("inst", None, "space", None),
        P("inst", "space", None),
        P("inst", "space", None),
        P("inst", "space", None),
        P("space", None),
        P(),
        P("inst", None, None),
        P(),
        P(),
        P(),
        P("space", None, None),
        P(None, "space", None),
        P("space", None, None),
        P("space", None),
    )
    out_specs = (P("inst", None, "space", None), P("inst", None, "space", None))
    return jax.shard_map(
        functools.partial(body, mesh.shape["space"]),
        mesh=mesh,
        in_specs=in_specs,
        out_specs=out_specs,
        check_vma=False,
    )
```
